128 devices in a mesh: gz: 32 (over y, x, core), gy: 4 (over z).
Axes of the slice: x: 4, y: 4, z: 4, core: 2. Of those that a mesh axis runs over, the one named last changes fastest.
Arguments:
- init: float32 [128, 2048, 512], P('gz', None, 'gy'), may hold values from -6 to 6
- measured: float32 [4, 128, 2048, 512], P(None, None, 'gz', 'gy'), may hold values from -70 to 70
- mask: int32 [32, 8], replicated, may hold values from 0 to 1, as said below
- kernel_index: int32 [4, 8, 32], replicated, may hold values from 0 to 15
- kernels: float32 [16, 31], replicated, may hold values from 0.02 to 0.3
Outputs:
- solved: float32 [128, 2048, 512], P('gz', None, 'gy')
The draws below stay inside these ranges and needn't reach their ends.
Inputs may be any that keep to these rules, and one draw needn't show every extreme that they name: `mask`: 1 marks a tissue block; in each aligned region of 64 x 128 lateral cells, whose blocks start at multiples of 64 and 128, exactly 1 block is 1.
All inputs are finite; a program needn't handle non-finite values.
Results may differ from the reference program's by a relative error of at most 0.0003.
Values sent between devices are 32-bit elements; how exact they have to be, the bound alone decides.
A program may use at most 128 MiB of HBM per device.

```python
import math
import jax
import jax.numpy as jnp
from jax import lax

NZ = 128
XT = 64
YD = 128
BX = 64
BY = 64
TISSUE = 1
ZBW = 16
TAPS = 31
VIEWS = 4
NK = 16
ITERS = 4
HALF = 15
ZBANDS = 8
NX = 2048
NY = 512
XBLOCKS = 32


def draw_measured(key, part):
    across = jnp.arange(NX, dtype=jnp.float32) / NX
    view_rates = 1.0 + jnp.arange(VIEWS, dtype=jnp.float32) / (VIEWS - 1.0)
    exponent = 0.5 * view_rates[:, None] * across[None, :]
    shape_full = (VIEWS, NZ, NX, NY)
    scale = 10.0 ** exponent
    base = jax.random.truncated_normal(key, -6.0, 6.0, shape_full, jnp.float32)
    return base * scale[:, None, :, None]


def draw_mask(key, part):
    tile_count = NX // XT
    groups = NY // YD
    across = XT // BX
    downward = YD // BY
    region_keys = jax.random.split(key, tile_count * groups)

    def one_region(region_key):
        return jax.random.permutation(region_key, across * downward)
    positions = jax.vmap(one_region)(region_keys)
    tissue_flags = (positions < TISSUE).astype(jnp.int32)
    tissue_flags = tissue_flags.reshape(tile_count, groups, across, downward).transpose(0, 2, 1, 3)
    return tissue_flags.reshape(tile_count * across, groups * downward)


def with_ends(result, stream_key, smallest, top_value):
    extent = result.shape
    index_at = [jax.random.randint(jax.random.fold_in(stream_key, axis), (), 0, extent[axis]) for axis in range(len(extent))]
    result = result.at[tuple(index_at)].set(smallest)
    longest = extent.index(max(extent))
    index_at[longest] = (index_at[longest] + 1) % extent[longest]
    return result.at[tuple(index_at)].set(top_value)


def levels(rng, extent, shards, smallest, largest):
    def one(axis_at, blocks):
        heights = jax.random.uniform(jax.random.fold_in(jax.random.fold_in(rng, 6), axis_at), (blocks,), jnp.float32, smallest / len(shards), largest / len(shards))
        return jnp.repeat(jnp.exp(heights), extent[axis_at] // blocks).reshape((-1,) + (1,) * (len(extent) - axis_at - 1))

    factor_of = one(*shards[0])
    for cut in shards[1:]:
        factor_of = factor_of * one(*cut)
    return factor_of


def normal_values(rng, shape, spread, bound, shards=(), kind=jnp.bfloat16):
    entries = spread * jax.random.normal(rng, shape, jnp.float32)
    if shards:
        entries = entries * levels(rng, shape, shards, -0.22, 0.18)
    return jnp.clip(entries, -bound, bound).astype(kind)


def setup_inputs(seed: int = 0) -> dict:
    streams_of = jax.random.split(jax.random.key(seed), 6)
    return {
        "init": normal_values(streams_of[0], (NZ, NX, NY), 1.0, 6.0, ((0, 32), (2, 4)), jnp.float32),
        "measured": draw_measured(jax.random.fold_in(streams_of[5], 71), 0),
        "mask": draw_mask(jax.random.fold_in(streams_of[5], 71), 0),
        "kernel_index": with_ends(jax.random.randint(streams_of[3], (VIEWS, ZBANDS, XBLOCKS), 0, NK), jax.random.fold_in(streams_of[3], 1), 0, NK - 1).astype(jnp.int32),
        "kernels": jnp.clip(jnp.exp(jax.random.uniform(streams_of[4], (NK, TAPS), jnp.float32, math.log(0.02), math.log(0.3))), 0.02, 0.3),
    }


HIGHEST = lax.Precision.HIGHEST
damping = 1.0


def blur_tables(kernel_index, kernels):
    onehot = (kernel_index[..., None] == jnp.arange(NK, dtype=jnp.int32)).astype(jnp.float32)
    tap_values = jnp.einsum("vabk,kt->vabt", onehot, kernels.astype(jnp.float32), precision=HIGHEST)
    row_taps = jnp.repeat(tap_values, ZBW, axis=1)
    depths = jnp.arange(NZ, dtype=jnp.int32)
    offset = depths[None, :] - depths[:, None] + HALF
    tap_select = (offset[:, :, None] == jnp.arange(TAPS, dtype=jnp.int32)).astype(jnp.float32)
    return jnp.einsum("vzbt,zwt->vbzw", row_taps, tap_select, precision=HIGHEST)


def reference(init, measured, mask, kernel_index, kernels):
    blur_mats = blur_tables(kernel_index, kernels)
    gram_mats = jnp.einsum("vbzw,vbzu->bwu", blur_mats, blur_mats, precision=HIGHEST)
    band_count = NX // BX
    projected = jnp.zeros((NZ, band_count, BX, NY), jnp.float32)
    for view_index in range(VIEWS):
        view_data = measured[view_index].reshape(NZ, band_count, BX, NY)
        projected = projected + jnp.einsum("bzw,zbxy->wbxy", blur_mats[view_index], view_data, precision=HIGHEST)
    projected = projected.reshape(NZ, NX, NY)
    tissue = jnp.repeat(jnp.repeat(mask.astype(jnp.float32), BX, axis=0), BY, axis=1)

    def apply_gram(field):
        product = jnp.einsum("bwz,zbxy->wbxy", gram_mats, field.reshape(NZ, band_count, BX, NY), precision=HIGHEST)
        return product.reshape(NZ, NX, NY)

    def operate(field):
        return damping * field + tissue * apply_gram(field)

    solved = init
    residual = tissue * (projected - apply_gram(init))
    direction = residual
    norm_now = jnp.sum(residual * residual)
    for iteration in range(ITERS):
        image_field = operate(direction)
        step_size = norm_now / jnp.sum(direction * image_field)
        solved = solved + step_size * direction
        residual = residual - step_size * image_field
        norm_next = jnp.sum(residual * residual)
        direction = residual + (norm_next / norm_now) * direction
        norm_now = norm_next
    return solved
```

```python
import jax
import jax.numpy as jnp
from jax import lax
from jax.experimental import pallas as pl
from jax.experimental.pallas import tpu as pltpu
from jax.sharding import PartitionSpec as P

NZ = 128
XT = 64
YD = 128
ZBW = 16
TAPS = 31
VIEWS = 4
NK = 16
ITERS = 4
HALF = 15
ZBANDS = 8
TILES = 32
RINGX, RINGY, CORES = 4, 4, 2
DEPTHS = 4
CHUNKS = 4
ROWS = 8
PIECE = DEPTHS * ROWS
PART = TILES * PIECE

MESH = pl.DeviceIdType.MESH
HIGHEST = lax.Precision.HIGHEST
F32 = jnp.float32
BF16 = jnp.bfloat16


def away(d, n):
    return min(d, n - d)


OFFSETS = sorted(
    ((dx, dy, dc) for dx in range(RINGX) for dy in range(RINGY) for dc in range(CORES)),
    key=lambda t: (-(away(t[0], RINGX) + away(t[1], RINGY)), t),
)
OFFSETS.remove((0, 0, 0))
FAR = len(OFFSETS)


def dot(a, b, precision=None):
    return jnp.dot(a, b, precision=precision, preferred_element_type=F32)


def dot_nt(a, b):
    return lax.dot_general(
        a, b, (((1,), (1,)), ((), ())), precision=HIGHEST, preferred_element_type=F32
    )


def halves(value):
    high = value.astype(BF16)
    return high, (value - high.astype(F32)).astype(BF16)


def pack(low_rows, high_rows, upper, lane):
    rolled = pltpu.roll(jnp.where(upper, low_rows, high_rows), 64, 1)
    return jnp.where(
        lane < 64, jnp.where(upper, rolled, low_rows), jnp.where(upper, high_rows, rolled)
    )


def mix(row, low_rows, high_rows, upper, lane):
    rolled = pltpu.roll(row, 64, 1)
    left = lane < 64
    spread_low = jnp.where(upper, rolled, row)
    spread_high = jnp.where(upper, row, rolled)
    tissue = jnp.logical_xor(left, upper)
    return jnp.where(tissue, spread_low, low_rows), jnp.where(tissue, spread_high, high_rows)


def cg_weights(moments, centre, half):
    product = [
        [0.5 * (moments[i + j] + moments[abs(i - j)]) for j in range(ITERS + 1)]
        for i in range(ITERS)
    ]

    def apply(a):
        out = [centre * value for value in a] + [None]

        def put(j, value):
            out[j] = value if out[j] is None else out[j] + value

        for j, value in enumerate(a):
            if j == 0:
                put(1, half * value)
            else:
                put(j + 1, 0.5 * half * value)
                put(j - 1, 0.5 * half * value)
        return out

    def square(a):
        total = None
        for i in range(len(a)):
            row = a[i] * product[i][i]
            for j in range(i + 1, len(a)):
                row = row + 2.0 * a[j] * product[i][j]
            total = a[i] * row if total is None else total + a[i] * row
        return total

    def inner(a, b):
        total = None
        for i in range(len(a)):
            row = None
            for j in range(len(b)):
                term = b[j] * product[i][j]
                row = term if row is None else row + term
            total = a[i] * row if total is None else total + a[i] * row
        return total

    one = jnp.ones_like(moments[0])
    residual, direction, step = [one], [one], []
    norm_now = moments[0]
    for iteration in range(ITERS):
        image = apply(direction)
        alpha = norm_now / inner(direction, image)
        step = [
            alpha * d if j >= len(step) else step[j] + alpha * d for j, d in enumerate(direction)
        ]
        if iteration == ITERS - 1:
            return step
        residual = [
            -alpha * v if j >= len(residual) else residual[j] - alpha * v
            for j, v in enumerate(image)
        ]
        norm_next = square(residual)
        ratio = norm_next / norm_now
        direction = [
            r if j >= len(direction) else r + ratio * direction[j] for j, r in enumerate(residual)
        ]
        norm_now = norm_next


def solve_kernel(
    init_ref, measured_ref, mask_ref, index_ref, index_row_ref, kernels_ref, prior,
    views, sent, field, back, solved, resid, taps, kpad, blur_rows, blur_ops, gram_ops, step_ops,
    cheb, total, part, part_z, part_g, sum_z,
    prior_sem, view_sem, send_sem, recv_sem, back_sem, ret_sem, z_send, z_recv, g_send, g_recv,
):
    me = lax.axis_index("gz")
    row = lax.axis_index("gy")
    my_core = lax.rem(me, CORES)
    my_x = lax.rem(lax.div(me, CORES), RINGX)
    my_y = lax.div(me, CORES * RINGX)

    def peer(offset):
        dx, dy, dc = offset
        return (
            lax.rem(my_y + dy, RINGY) * RINGX + lax.rem(my_x + dx, RINGX)
        ) * CORES + lax.rem(my_core + dc, CORES)

    def prior_copy(d):
        return pltpu.make_async_copy(init_ref.at[d], prior.at[d], prior_sem.at[d])

    def view_copy(i):
        return pltpu.make_async_copy(
            measured_ref.at[:, pl.ds(i * ROWS, ROWS), :], views.at[i], view_sem.at[i]
        )

    for d in range(DEPTHS):
        prior_copy(d).start()

    barrier = pltpu.get_barrier_semaphore()
    for offset in OFFSETS:
        pl.semaphore_signal(barrier, inc=1, device_id=(peer(offset), row), device_id_type=MESH)
    for dz in range(1, 4):
        pl.semaphore_signal(
            barrier, inc=1, device_id=(me, lax.rem(row + dz, 4)), device_id_type=MESH
        )

    lane8 = lax.broadcasted_iota(jnp.int32, (ROWS, 128), 1)
    for d in range(DEPTHS):
        prior_copy(d).wait()
    for c in range(CHUNKS):
        for i in (c, c + CHUNKS):
            view_copy(i).start()

    def pack_chunk(c):
        @pl.loop(0, TILES)
        def _(p):
            upper = jnp.full((ROWS, 128), mask_ref[2 * row + 1, p], jnp.int32) != 0
            for d in range(DEPTHS):
                low = pl.multiple_of(p * XT + c * ROWS, ROWS)
                high = pl.multiple_of(p * XT + c * ROWS + XT // 2, ROWS)
                packed = pack(
                    prior[d, pl.ds(low, ROWS), :], prior[d, pl.ds(high, ROWS), :], upper, lane8
                )
                sent[c, pl.ds(pl.multiple_of(p * PIECE + d * ROWS, ROWS), ROWS), :] = packed

    def send_chunk(source, target, c, send, recv):
        for offset in OFFSETS:
            p = peer(offset)
            pltpu.make_async_remote_copy(
                src_ref=source.at[c, pl.ds(pl.multiple_of(p * PIECE, PIECE), PIECE)],
                dst_ref=target.at[c, pl.ds(pl.multiple_of(me * PIECE, PIECE), PIECE)],
                send_sem=send.at[c],
                recv_sem=recv.at[c],
                device_id=(p, row),
                device_id_type=MESH,
            ).start()

    def chunk_copy(source, target, c, send, recv):
        return pltpu.make_async_remote_copy(
            src_ref=source.at[c, pl.ds(0, FAR * PIECE)],
            dst_ref=target.at[c, pl.ds(0, FAR * PIECE)],
            send_sem=send.at[c],
            recv_sem=recv.at[c],
            device_id=(peer(OFFSETS[0]), row),
            device_id_type=MESH,
        )

    pack_chunk(0)
    pl.semaphore_wait(barrier, FAR + 3)

    @pl.loop(0, CHUNKS)
    def _(c):
        send_chunk(sent, field, c, send_sem, recv_sem)

        @pl.when(c < CHUNKS - 1)
        def _():
            pack_chunk(c + 1)

    own = pl.ds(pl.multiple_of(me * PIECE, PIECE), PIECE)
    for c in range(CHUNKS):
        field[c, own, :] = sent[c, own, :]

    lane = lax.broadcasted_iota(jnp.int32, (NZ, NZ), 1)
    depth = lax.broadcasted_iota(jnp.int32, (NZ, NZ), 0)
    kpad[...] = jnp.zeros((NK, 128), F32)
    kpad[:, 0:TAPS] = kernels_ref[...]
    for v in range(VIEWS):
        for band in range(ZBANDS):
            k = index_ref[v * ZBANDS + band, me]
            taps[pl.ds((v * ZBANDS + band) * ZBW, ZBW), :] = jnp.broadcast_to(
                kpad[pl.ds(k, 1), :], (ZBW, 128)
            )
    near = jnp.abs(lane - depth) <= HALF
    for v in range(VIEWS):
        at = pl.ds(v * NZ, NZ)
        mat = jnp.where(
            near, pltpu.roll(taps[at, :], 128 - HALF, 1, stride=1, stride_axis=0), 0.0
        )
        turned = mat.T
        blur_rows[at, :] = mat
        high, low = halves(turned)
        blur_ops[0:NZ, at] = high
        blur_ops[NZ:, at] = low
        taps[at, :] = turned
    grams = dot(taps[0:NZ, :], blur_rows[0:NZ, :], HIGHEST)
    for v in range(1, VIEWS):
        at = pl.ds(v * NZ, NZ)
        grams = grams + dot(taps[at, :], blur_rows[at, :], HIGHEST)
    high, low = halves(grams)
    gram_ops[0:NZ, 0:NZ] = high
    gram_ops[0:NZ, NZ:] = high
    gram_ops[NZ:, 0:NZ] = low
    gram_ops[NZ:, NZ:] = jnp.zeros((NZ, NZ), BF16)

    bins = lax.broadcasted_iota(jnp.int32, (NK, TILES), 0)
    span = lax.broadcasted_iota(jnp.int32, (3 * ZBW, 128), 0)
    tap = lax.broadcasted_iota(jnp.int32, (3 * ZBW, 128), 1)
    window = jnp.where(jnp.logical_and(tap >= span - ZBW, tap < span), 1.0, 0.0)
    sums = dot_nt(window, kpad[...]) * dot_nt(jnp.ones((3 * ZBW, 128), F32), kpad[...])
    spreads = []
    for band in range(ZBANDS):
        counts = jnp.zeros((NK, TILES), F32)
        for v in range(VIEWS):
            at = v * ZBANDS + band
            counts = counts + jnp.where(index_row_ref[at : at + 1, :] == bins, 1.0, 0.0)
        spreads.append(dot(sums, counts, HIGHEST))
    row_sums = None
    for band in range(ZBANDS):
        here = spreads[band][ZBW : 2 * ZBW, :]
        if band > 0:
            here = here + spreads[band - 1][2 * ZBW :, :]
        if band < ZBANDS - 1:
            here = here + spreads[band + 1][0:ZBW, :]
        row_sums = here if row_sums is None else jnp.maximum(row_sums, here)
    bound = jnp.max(jnp.max(row_sums, axis=0, keepdims=True), axis=1, keepdims=True)
    half = jnp.broadcast_to(0.5001 * bound, (1, 128))
    centre = 1.0 + half

    eye = jnp.where(lane == depth, 1.0, 0.0)
    cheb[0] = eye
    cheb[1] = grams / half - eye
    cheb[2] = 2.0 * dot(cheb[1], cheb[1], HIGHEST) - eye
    cheb[3] = 2.0 * dot(cheb[1], cheb[2], HIGHEST) - cheb[1]
    cheb[4] = 2.0 * dot(cheb[2], cheb[2], HIGHEST) - eye
    cheb[5] = 2.0 * dot(cheb[2], cheb[3], HIGHEST) - cheb[1]
    cheb[6] = 2.0 * dot(cheb[3], cheb[3], HIGHEST) - eye
    cheb[7] = 2.0 * dot(cheb[3], cheb[4], HIGHEST) - cheb[1]

    mine = jnp.full((NZ, 128), mask_ref[2 * row + 1, me], jnp.int32) != 0

    for i in range(2 * CHUNKS):
        view_copy(i).wait()

    @pl.loop(0, CHUNKS)
    def _(c):
        @pl.loop(0, ROWS // 2)
        def _(pair):
            product = None
            for v in range(VIEWS):
                sides = []
                for r in range(2):
                    at = pl.ds(pair * 2 + r, NZ, stride=ROWS)
                    lows = views.at[c, pl.ds(v * NZ, NZ)].reshape(NZ * ROWS, 128)[at, :]
                    highs = views.at[c + CHUNKS, pl.ds(v * NZ, NZ)].reshape(NZ * ROWS, 128)[at, :]
                    sides.append(pack(lows, highs, mine, lane))
                high, low = halves(jnp.concatenate(sides, axis=1))
                ops = blur_ops[:, pl.ds(v * NZ, NZ)]
                both = dot(ops, high)
                term = both[0:NZ] + both[NZ:] + dot(ops[0:NZ], low)
                product = term if product is None else product + term
            resid[c * (ROWS // 2) + pair] = product

    def columns(c, pair):
        sides = [field[c, pl.ds(pair * 2 + r, NZ, stride=ROWS), :] for r in range(2)]
        return jnp.concatenate(sides, axis=1)

    def times(ops, value):
        high, low = halves(value)
        both = dot(ops[...], jnp.concatenate([high, low], axis=0))
        return both[0:NZ] + both[NZ:]

    total[...] = jnp.zeros((NZ, NZ), F32)

    @pl.loop(0, CHUNKS)
    def _(c):
        chunk_copy(sent, field, c, send_sem, recv_sem).wait_recv()

        @pl.loop(0, ROWS // 2)
        def _(pair):
            at = c * (ROWS // 2) + pair
            first = resid[at] - times(gram_ops, columns(c, pair))
            resid[at] = first
            total[...] += dot_nt(first, first)

    lane1 = lax.broadcasted_iota(jnp.int32, (1, 128), 1)
    local = jnp.zeros((1, 128), F32)
    for k in range(2 * ITERS):
        value = jnp.sum(cheb[k] * total[...], axis=0, keepdims=True)
        local = jnp.where(lane1 == k, jnp.sum(value, axis=1, keepdims=True), local)
    part[0] = local
    part_z[row] = local
    hops = []
    for dz in range(1, 4):
        copy = pltpu.make_async_remote_copy(
            src_ref=part.at[0],
            dst_ref=part_z.at[row],
            send_sem=z_send.at[dz - 1],
            recv_sem=z_recv.at[dz - 1],
            device_id=(me, lax.rem(row + dz, 4)),
            device_id_type=MESH,
        )
        copy.start()
        hops.append(copy)
    for copy in hops:
        copy.wait()
    along = (part_z[0] + part_z[1]) + (part_z[2] + part_z[3])
    sum_z[0] = along
    part_g[me] = along
    for offset in OFFSETS:
        p = peer(offset)
        pltpu.make_async_remote_copy(
            src_ref=sum_z.at[0],
            dst_ref=part_g.at[me],
            send_sem=g_send.at[0],
            recv_sem=g_recv.at[0],
            device_id=(p, row),
            device_id_type=MESH,
        ).start()
    everyone = pltpu.make_async_remote_copy(
        src_ref=part_g.at[pl.ds(0, FAR)],
        dst_ref=part_g.at[pl.ds(0, FAR)],
        send_sem=g_send.at[0],
        recv_sem=g_recv.at[0],
        device_id=(peer(OFFSETS[0]), row),
        device_id_type=MESH,
    )
    everyone.wait_recv()
    whole = jnp.sum(part_g[...], axis=0)
    moments = [
        jnp.broadcast_to(
            jnp.sum(jnp.where(lane1 == k, whole, 0.0), axis=1, keepdims=True), (1, 128)
        )
        for k in range(2 * ITERS)
    ]
    weights = cg_weights(moments, centre, half)

    poly = weights[0] * cheb[0]
    for j in range(1, ITERS):
        poly = poly + weights[j] * cheb[j]
    high, low = halves(poly)
    step_ops[0:NZ, 0:NZ] = high
    step_ops[0:NZ, NZ:] = high
    step_ops[NZ:, 0:NZ] = low
    step_ops[NZ:, NZ:] = jnp.zeros((NZ, NZ), BF16)

    @pl.loop(0, CHUNKS)
    def _(c):
        @pl.loop(0, ROWS // 2)
        def _(pair):
            moved = columns(c, pair) + times(step_ops, resid[c * (ROWS // 2) + pair])
            for r in range(2):
                back[c, pl.ds(pair * 2 + r, NZ, stride=ROWS), :] = moved[:, r * 128 : (r + 1) * 128]

        solved[c, own, :] = back[c, own, :]
        send_chunk(back, solved, c, back_sem, ret_sem)

    @pl.loop(0, CHUNKS)
    def _(c):
        chunk_copy(back, solved, c, back_sem, ret_sem).wait_recv()

        @pl.loop(0, TILES)
        def _(b):
            upper = jnp.full((ROWS, 128), mask_ref[2 * row + 1, b], jnp.int32) != 0
            for d in range(DEPTHS):
                low = pl.ds(pl.multiple_of(b * XT + c * ROWS, ROWS), ROWS)
                high = pl.ds(pl.multiple_of(b * XT + c * ROWS + XT // 2, ROWS), ROWS)
                prior[d, low, :], prior[d, high, :] = mix(
                    solved[c, pl.ds(pl.multiple_of(b * PIECE + d * ROWS, ROWS), ROWS), :],
                    prior[d, low, :], prior[d, high, :], upper, lane8,
                )

    everyone.wait_send()
    for c in range(CHUNKS):
        chunk_copy(sent, field, c, send_sem, recv_sem).wait_send()
        chunk_copy(back, solved, c, back_sem, ret_sem).wait_send()


def place_kernel(solved_ref, out_ref, sem):
    copies = [pltpu.make_async_copy(solved_ref.at[d], out_ref.at[d], sem.at[d]) for d in range(DEPTHS)]
    for copy in copies:
        copy.start()
    for copy in copies:
        copy.wait()


def local(init, measured, mask, kernel_index, kernels):
    nx = TILES * XT
    smem = pl.BlockSpec(memory_space=pltpu.SMEM)
    vmem = pl.BlockSpec(memory_space=pltpu.VMEM)
    hbm = pl.BlockSpec(memory_space=pltpu.HBM)
    dma = pltpu.SemaphoreType.DMA
    solved = pl.pallas_call(
        solve_kernel,
        out_shape=jax.ShapeDtypeStruct((DEPTHS, nx, 128), F32),
        in_specs=[hbm, hbm, smem, smem, vmem, vmem],
        out_specs=vmem,
        scratch_shapes=[
            pltpu.VMEM((2 * CHUNKS, VIEWS * NZ, ROWS, 128), F32),
            pltpu.VMEM((CHUNKS, PART, 128), F32),
            pltpu.VMEM((CHUNKS, PART, 128), F32),
            pltpu.VMEM((CHUNKS, PART, 128), F32),
            pltpu.VMEM((CHUNKS, PART, 128), F32),
            pltpu.VMEM((CHUNKS * ROWS // 2, NZ, 256), F32),
            pltpu.VMEM((VIEWS * NZ, 128), F32),
            pltpu.VMEM((NK, 128), F32),
            pltpu.VMEM((VIEWS * NZ, NZ), F32),
            pltpu.VMEM((2 * NZ, VIEWS * NZ), BF16),
            pltpu.VMEM((2 * NZ, 2 * NZ), BF16),
            pltpu.VMEM((2 * NZ, 2 * NZ), BF16),
            pltpu.VMEM((2 * ITERS, NZ, NZ), F32),
            pltpu.VMEM((NZ, NZ), F32),
            pltpu.VMEM((1, 1, 128), F32),
            pltpu.VMEM((4, 1, 128), F32),
            pltpu.VMEM((TILES, 1, 128), F32),
            pltpu.VMEM((1, 1, 128), F32),
            dma((DEPTHS,)),
            dma((2 * CHUNKS,)),
            dma((CHUNKS,)),
            dma((CHUNKS,)),
            dma((CHUNKS,)),
            dma((CHUNKS,)),
            dma((3,)),
            dma((3,)),
            dma((1,)),
            dma((1,)),
        ],
        compiler_params=pltpu.CompilerParams(
            collective_id=0, has_side_effects=True, vmem_limit_bytes=48 << 20
        ),
        name="solve",
    )(
        init,
        measured.reshape(VIEWS * NZ, XT, YD),
        mask.T,
        kernel_index.reshape(VIEWS * ZBANDS, TILES),
        kernel_index.reshape(VIEWS * ZBANDS, TILES),
        kernels,
    )
    return pl.pallas_call(
        place_kernel,
        out_shape=jax.ShapeDtypeStruct((DEPTHS, nx, 128), F32),
        in_specs=[vmem],
        out_specs=hbm,
        scratch_shapes=[dma((DEPTHS,))],
        compiler_params=pltpu.CompilerParams(vmem_limit_bytes=8 << 20),
        name="place",
    )(solved)


def solution(mesh):
    return jax.shard_map(
        local,
        mesh=mesh,
        in_specs=(P("gz", None, "gy"), P(None, None, "gz", "gy"), P(), P(), P()),
        out_specs=P("gz", None, "gy"),
        check_vma=False,
    )
```

```python
import jax
import jax.numpy as jnp
from jax import lax
from jax.experimental import pallas as pl
from jax.experimental.pallas import tpu as pltpu
from jax.sharding import PartitionSpec as P

NZ = 128
XT = 64
YD = 128
ZBW = 16
TAPS = 31
VIEWS = 4
NK = 16
ITERS = 4
HALF = 15
ZBANDS = 8
NY_BLOCKS = 8
TILES = 32
RINGX, RINGY, CORES = 4, 4, 2
DEPTHS = 4
CHUNKS = 4
ROWS = 8
PIECE = DEPTHS * ROWS
PART = TILES * PIECE

MESH = pl.DeviceIdType.MESH
HIGHEST = lax.Precision.HIGHEST
F32 = jnp.float32
BF16 = jnp.bfloat16


def away(d, n):
    return min(d, n - d)


OFFSETS = sorted(
    ((dx, dy, dc) for dx in range(RINGX) for dy in range(RINGY) for dc in range(CORES)),
    key=lambda t: (-(away(t[0], RINGX) + away(t[1], RINGY)), t),
)
OFFSETS.remove((0, 0, 0))
FAR = len(OFFSETS)


def dot(a, b, precision=None):
    return jnp.dot(a, b, precision=precision, preferred_element_type=F32)


def dot_nt(a, b):
    return lax.dot_general(
        a, b, (((1,), (1,)), ((), ())), precision=HIGHEST, preferred_element_type=F32
    )


def halves(value):
    high = value.astype(BF16)
    return high, (value - high.astype(F32)).astype(BF16)


def pack(low_rows, high_rows, upper, lane):
    rolled = pltpu.roll(jnp.where(upper, low_rows, high_rows), 64, 1)
    return jnp.where(
        lane < 64, jnp.where(upper, rolled, low_rows), jnp.where(upper, high_rows, rolled)
    )


def mix(row, low_rows, high_rows, upper, lane):
    rolled = pltpu.roll(row, 64, 1)
    left = lane < 64
    spread_low = jnp.where(upper, rolled, row)
    spread_high = jnp.where(upper, row, rolled)
    tissue = jnp.logical_xor(left, upper)
    return jnp.where(tissue, spread_low, low_rows), jnp.where(tissue, spread_high, high_rows)


def cg_weights(moments, centre, half):
    product = [
        [0.5 * (moments[i + j] + moments[abs(i - j)]) for j in range(ITERS + 1)]
        for i in range(ITERS)
    ]

    def apply(a):
        out = [centre * value for value in a] + [None]

        def put(j, value):
            out[j] = value if out[j] is None else out[j] + value

        for j, value in enumerate(a):
            if j == 0:
                put(1, half * value)
            else:
                put(j + 1, 0.5 * half * value)
                put(j - 1, 0.5 * half * value)
        return out

    def square(a):
        total = None
        for i in range(len(a)):
            row = a[i] * product[i][i]
            for j in range(i + 1, len(a)):
                row = row + 2.0 * a[j] * product[i][j]
            total = a[i] * row if total is None else total + a[i] * row
        return total

    def inner(a, b):
        total = None
        for i in range(len(a)):
            row = None
            for j in range(len(b)):
                term = b[j] * product[i][j]
                row = term if row is None else row + term
            total = a[i] * row if total is None else total + a[i] * row
        return total

    one = jnp.ones_like(moments[0])
    residual, direction, step = [one], [one], []
    norm_now = moments[0]
    for iteration in range(ITERS):
        image = apply(direction)
        alpha = norm_now / inner(direction, image)
        step = [
            alpha * d if j >= len(step) else step[j] + alpha * d for j, d in enumerate(direction)
        ]
        if iteration == ITERS - 1:
            return step
        residual = [
            -alpha * v if j >= len(residual) else residual[j] - alpha * v
            for j, v in enumerate(image)
        ]
        norm_next = square(residual)
        ratio = norm_next / norm_now
        direction = [
            r if j >= len(direction) else r + ratio * direction[j] for j, r in enumerate(residual)
        ]
        norm_now = norm_next


def solve_kernel(
    init_ref, measured_ref, mask_hbm, index_hbm, kernels_hbm, prior,
    mask_ref, index_ref, index_row_ref, kernels_ref, views, sent, field, back, solved, resid, stacks, taps, kpad, blur_rows, blur_ops, gram_ops, step_ops,
    cheb, total, part, part_z, part_g, sum_z,
    small_sem, prior_sem, view_sem, send_sem, recv_sem, back_sem, ret_sem, z_send, z_recv, g_send, g_recv,
):
    me = lax.axis_index("gz")
    row = lax.axis_index("gy")
    my_core = lax.rem(me, CORES)
    my_x = lax.rem(lax.div(me, CORES), RINGX)
    my_y = lax.div(me, CORES * RINGX)

    def peer(offset):
        dx, dy, dc = offset
        return (
            lax.rem(my_y + dy, RINGY) * RINGX + lax.rem(my_x + dx, RINGX)
        ) * CORES + lax.rem(my_core + dc, CORES)

    def prior_copy(d):
        return pltpu.make_async_copy(init_ref.at[d], prior.at[d], prior_sem.at[d])

    def view_copy(i):
        return pltpu.make_async_copy(
            measured_ref.at[:, pl.ds(i * ROWS, ROWS), :], views.at[i], view_sem.at[i]
        )

    small = [
        pltpu.make_async_copy(source, target, small_sem.at[i])
        for i, (source, target) in enumerate(
            (
                (mask_hbm, mask_ref),
                (index_hbm, index_ref),
                (index_hbm, index_row_ref),
                (kernels_hbm, kernels_ref),
            )
        )
    ]
    for copy in small[:1]:
        copy.start()
    for d in range(DEPTHS):
        prior_copy(d).start()
    for copy in small[1:]:
        copy.start()

    barrier = pltpu.get_barrier_semaphore()
    for offset in OFFSETS:
        pl.semaphore_signal(barrier, inc=1, device_id=(peer(offset), row), device_id_type=MESH)
    for dz in range(1, 4):
        pl.semaphore_signal(
            barrier, inc=1, device_id=(me, lax.rem(row + dz, 4)), device_id_type=MESH
        )

    lane8 = lax.broadcasted_iota(jnp.int32, (ROWS, 128), 1)
    for copy in small:
        copy.wait()
    for d in range(DEPTHS):
        prior_copy(d).wait()
    for c in range(CHUNKS):
        for i in (c, c + CHUNKS):
            view_copy(i).start()

    def pack_chunk(c):
        @pl.loop(0, TILES)
        def _(p):
            upper = jnp.full((ROWS, 128), mask_ref[2 * row + 1, p], jnp.int32) != 0
            for d in range(DEPTHS):
                low = pl.multiple_of(p * XT + c * ROWS, ROWS)
                high = pl.multiple_of(p * XT + c * ROWS + XT // 2, ROWS)
                packed = pack(
                    prior[d, pl.ds(low, ROWS), :], prior[d, pl.ds(high, ROWS), :], upper, lane8
                )
                sent[c, pl.ds(pl.multiple_of(p * PIECE + d * ROWS, ROWS), ROWS), :] = packed

    def send_chunk(source, target, c, send, recv):
        for offset in OFFSETS:
            p = peer(offset)
            pltpu.make_async_remote_copy(
                src_ref=source.at[c, pl.ds(pl.multiple_of(p * PIECE, PIECE), PIECE)],
                dst_ref=target.at[c, pl.ds(pl.multiple_of(me * PIECE, PIECE), PIECE)],
                send_sem=send.at[c],
                recv_sem=recv.at[c],
                device_id=(p, row),
                device_id_type=MESH,
            ).start()

    def chunk_copy(source, target, c, send, recv):
        return pltpu.make_async_remote_copy(
            src_ref=source.at[c, pl.ds(0, FAR * PIECE)],
            dst_ref=target.at[c, pl.ds(0, FAR * PIECE)],
            send_sem=send.at[c],
            recv_sem=recv.at[c],
            device_id=(peer(OFFSETS[0]), row),
            device_id_type=MESH,
        )

    pack_chunk(0)
    pl.semaphore_wait(barrier, FAR + 3)

    @pl.loop(0, CHUNKS)
    def _(c):
        send_chunk(sent, field, c, send_sem, recv_sem)

        @pl.when(c < CHUNKS - 1)
        def _():
            pack_chunk(c + 1)

    own = pl.ds(pl.multiple_of(me * PIECE, PIECE), PIECE)
    for c in range(CHUNKS):
        field[c, own, :] = sent[c, own, :]

    lane = lax.broadcasted_iota(jnp.int32, (NZ, NZ), 1)
    depth = lax.broadcasted_iota(jnp.int32, (NZ, NZ), 0)
    kpad[...] = jnp.zeros((NK, 128), F32)
    kpad[:, 0:TAPS] = kernels_ref[...]
    for v in range(VIEWS):
        for band in range(ZBANDS):
            k = index_ref[v * ZBANDS + band, me]
            taps[pl.ds((v * ZBANDS + band) * ZBW, ZBW), :] = jnp.broadcast_to(
                kpad[pl.ds(k, 1), :], (ZBW, 128)
            )
    near = jnp.abs(lane - depth) <= HALF
    for v in range(VIEWS):
        at = pl.ds(v * NZ, NZ)
        mat = jnp.where(
            near, pltpu.roll(taps[at, :], 128 - HALF, 1, stride=1, stride_axis=0), 0.0
        )
        turned = mat.T
        blur_rows[at, :] = mat
        high, low = halves(turned)
        blur_ops[0:NZ, at] = high
        blur_ops[NZ:, at] = low
        taps[at, :] = turned
    grams = dot(taps[0:NZ, :], blur_rows[0:NZ, :], HIGHEST)
    for v in range(1, VIEWS):
        at = pl.ds(v * NZ, NZ)
        grams = grams + dot(taps[at, :], blur_rows[at, :], HIGHEST)
    high, low = halves(grams)
    gram_ops[0:NZ, 0:NZ] = high
    gram_ops[0:NZ, NZ:] = high
    gram_ops[NZ:, 0:NZ] = low
    gram_ops[NZ:, NZ:] = jnp.zeros((NZ, NZ), BF16)

    bins = lax.broadcasted_iota(jnp.int32, (NK, TILES), 0)
    span = lax.broadcasted_iota(jnp.int32, (3 * ZBW, 128), 0)
    tap = lax.broadcasted_iota(jnp.int32, (3 * ZBW, 128), 1)
    window = jnp.where(jnp.logical_and(tap >= span - ZBW, tap < span), 1.0, 0.0)
    sums = dot_nt(window, kpad[...]) * dot_nt(jnp.ones((3 * ZBW, 128), F32), kpad[...])
    spreads = []
    for band in range(ZBANDS):
        counts = jnp.zeros((NK, TILES), F32)
        for v in range(VIEWS):
            at = v * ZBANDS + band
            counts = counts + jnp.where(index_row_ref[at : at + 1, :] == bins, 1.0, 0.0)
        spreads.append(dot(sums, counts, HIGHEST))
    row_sums = None
    for band in range(ZBANDS):
        here = spreads[band][ZBW : 2 * ZBW, :]
        if band > 0:
            here = here + spreads[band - 1][2 * ZBW :, :]
        if band < ZBANDS - 1:
            here = here + spreads[band + 1][0:ZBW, :]
        row_sums = here if row_sums is None else jnp.maximum(row_sums, here)
    bound = jnp.max(jnp.max(row_sums, axis=0, keepdims=True), axis=1, keepdims=True)
    half = jnp.broadcast_to(0.5001 * bound, (1, 128))
    centre = 1.0 + half

    eye = jnp.where(lane == depth, 1.0, 0.0)
    cheb[0] = eye
    cheb[1] = grams / half - eye
    cheb[2] = 2.0 * dot(cheb[1], cheb[1], HIGHEST) - eye
    cheb[3] = 2.0 * dot(cheb[1], cheb[2], HIGHEST) - cheb[1]
    cheb[4] = 2.0 * dot(cheb[2], cheb[2], HIGHEST) - eye
    cheb[5] = 2.0 * dot(cheb[2], cheb[3], HIGHEST) - cheb[1]
    cheb[6] = 2.0 * dot(cheb[3], cheb[3], HIGHEST) - eye
    cheb[7] = 2.0 * dot(cheb[3], cheb[4], HIGHEST) - cheb[1]

    mine = jnp.full((NZ, 128), mask_ref[2 * row + 1, me], jnp.int32) != 0

    for i in range(2 * CHUNKS):
        view_copy(i).wait()

    @pl.loop(0, CHUNKS)
    def _(c):
        @pl.loop(0, ROWS // 2)
        def _(pair):
            product = None
            for v in range(VIEWS):
                sides = []
                for r in range(2):
                    at = pl.ds(pair * 2 + r, NZ, stride=ROWS)
                    lows = views.at[c, pl.ds(v * NZ, NZ)].reshape(NZ * ROWS, 128)[at, :]
                    highs = views.at[c + CHUNKS, pl.ds(v * NZ, NZ)].reshape(NZ * ROWS, 128)[at, :]
                    sides.append(pack(lows, highs, mine, lane))
                high, low = halves(jnp.concatenate(sides, axis=1))
                ops = blur_ops[:, pl.ds(v * NZ, NZ)]
                both = dot(ops, high)
                term = both[0:NZ] + both[NZ:] + dot(ops[0:NZ], low)
                product = term if product is None else product + term
            resid[c * (ROWS // 2) + pair] = product

    def columns(c, pair):
        sides = [field[c, pl.ds(pair * 2 + r, NZ, stride=ROWS), :] for r in range(2)]
        return jnp.concatenate(sides, axis=1)

    def stacked(value):
        return jnp.concatenate(halves(value), axis=0)

    def times(ops, stack):
        both = dot(ops[...], stack)
        return both[0:NZ] + both[NZ:]

    total[...] = jnp.zeros((2 * NZ, 2 * NZ), F32)

    @pl.loop(0, CHUNKS)
    def _(c):
        chunk_copy(sent, field, c, send_sem, recv_sem).wait_recv()

        @pl.loop(0, ROWS // 2)
        def _(pair):
            at = c * (ROWS // 2) + pair
            first = resid[at] - times(gram_ops, stacked(columns(c, pair)))
            stack = stacked(first)
            stacks[at] = stack
            total[...] += lax.dot_general(
                stack, stack, (((1,), (1,)), ((), ())), preferred_element_type=F32
            )

    lane1 = lax.broadcasted_iota(jnp.int32, (1, 128), 1)
    local = jnp.zeros((1, 128), F32)
    square = total[0:NZ, 0:NZ] + (total[0:NZ, NZ:] + total[NZ:, 0:NZ]) + total[NZ:, NZ:]
    for k in range(2 * ITERS):
        value = jnp.sum(cheb[k] * square, axis=0, keepdims=True)
        local = jnp.where(lane1 == k, jnp.sum(value, axis=1, keepdims=True), local)
    part[0] = local
    part_z[row] = local
    hops = []
    for dz in range(1, 4):
        copy = pltpu.make_async_remote_copy(
            src_ref=part.at[0],
            dst_ref=part_z.at[row],
            send_sem=z_send.at[dz - 1],
            recv_sem=z_recv.at[dz - 1],
            device_id=(me, lax.rem(row + dz, 4)),
            device_id_type=MESH,
        )
        copy.start()
        hops.append(copy)
    for copy in hops:
        copy.wait()
    along = (part_z[0] + part_z[1]) + (part_z[2] + part_z[3])
    sum_z[0] = along
    part_g[me] = along
    for offset in OFFSETS:
        p = peer(offset)
        pltpu.make_async_remote_copy(
            src_ref=sum_z.at[0],
            dst_ref=part_g.at[me],
            send_sem=g_send.at[0],
            recv_sem=g_recv.at[0],
            device_id=(p, row),
            device_id_type=MESH,
        ).start()
    everyone = pltpu.make_async_remote_copy(
        src_ref=part_g.at[pl.ds(0, FAR)],
        dst_ref=part_g.at[pl.ds(0, FAR)],
        send_sem=g_send.at[0],
        recv_sem=g_recv.at[0],
        device_id=(peer(OFFSETS[0]), row),
        device_id_type=MESH,
    )
    everyone.wait_recv()
    whole = jnp.sum(part_g[...], axis=0)
    moments = [
        jnp.broadcast_to(
            jnp.sum(jnp.where(lane1 == k, whole, 0.0), axis=1, keepdims=True), (1, 128)
        )
        for k in range(2 * ITERS)
    ]
    weights = cg_weights(moments, centre, half)

    poly = weights[0] * cheb[0]
    for j in range(1, ITERS):
        poly = poly + weights[j] * cheb[j]
    high, low = halves(poly)
    step_ops[0:NZ, 0:NZ] = high
    step_ops[0:NZ, NZ:] = high
    step_ops[NZ:, 0:NZ] = low
    step_ops[NZ:, NZ:] = jnp.zeros((NZ, NZ), BF16)

    @pl.loop(0, CHUNKS)
    def _(c):
        @pl.loop(0, ROWS // 2)
        def _(pair):
            moved = columns(c, pair) + times(step_ops, stacks[c * (ROWS // 2) + pair])
            for r in range(2):
                back[c, pl.ds(pair * 2 + r, NZ, stride=ROWS), :] = moved[:, r * 128 : (r + 1) * 128]

        solved[c, own, :] = back[c, own, :]
        send_chunk(back, solved, c, back_sem, ret_sem)

    @pl.loop(0, CHUNKS)
    def _(c):
        chunk_copy(back, solved, c, back_sem, ret_sem).wait_recv()

        @pl.loop(0, TILES)
        def _(b):
            upper = jnp.full((ROWS, 128), mask_ref[2 * row + 1, b], jnp.int32) != 0
            for d in range(DEPTHS):
                low = pl.ds(pl.multiple_of(b * XT + c * ROWS, ROWS), ROWS)
                high = pl.ds(pl.multiple_of(b * XT + c * ROWS + XT // 2, ROWS), ROWS)
                prior[d, low, :], prior[d, high, :] = mix(
                    solved[c, pl.ds(pl.multiple_of(b * PIECE + d * ROWS, ROWS), ROWS), :],
                    prior[d, low, :], prior[d, high, :], upper, lane8,
                )

    everyone.wait_send()
    for c in range(CHUNKS):
        chunk_copy(sent, field, c, send_sem, recv_sem).wait_send()
        chunk_copy(back, solved, c, back_sem, ret_sem).wait_send()


def place_kernel(solved_ref, out_ref, sem):
    part = TILES * XT // 4
    copies = [
        pltpu.make_async_copy(
            solved_ref.at[d, pl.ds(i * part, part)],
            out_ref.at[d, pl.ds(i * part, part)],
            sem.at[d * 4 + i],
        )
        for d in range(DEPTHS)
        for i in range(4)
    ]
    for copy in copies:
        copy.start()
    for copy in copies:
        copy.wait()


def local(init, measured, mask, kernel_index, kernels):
    nx = TILES * XT
    vmem = pl.BlockSpec(memory_space=pltpu.VMEM)
    hbm = pl.BlockSpec(memory_space=pltpu.HBM)
    dma = pltpu.SemaphoreType.DMA
    solved = pl.pallas_call(
        solve_kernel,
        out_shape=jax.ShapeDtypeStruct((DEPTHS, nx, 128), F32),
        in_specs=[hbm] * 5,
        out_specs=vmem,
        scratch_shapes=[
            pltpu.SMEM((NY_BLOCKS, TILES), jnp.int32),
            pltpu.SMEM((VIEWS * ZBANDS, TILES), jnp.int32),
            pltpu.VMEM((VIEWS * ZBANDS, TILES), jnp.int32),
            pltpu.VMEM((NK, TAPS), F32),
            pltpu.VMEM((2 * CHUNKS, VIEWS * NZ, ROWS, 128), F32),
            pltpu.VMEM((CHUNKS, PART, 128), F32),
            pltpu.VMEM((CHUNKS, PART, 128), F32),
            pltpu.VMEM((CHUNKS, PART, 128), F32),
            pltpu.VMEM((CHUNKS, PART, 128), F32),
            pltpu.VMEM((CHUNKS * ROWS // 2, NZ, 256), F32),
            pltpu.VMEM((CHUNKS * ROWS // 2, 2 * NZ, 256), BF16),
            pltpu.VMEM((VIEWS * NZ, 128), F32),
            pltpu.VMEM((NK, 128), F32),
            pltpu.VMEM((VIEWS * NZ, NZ), F32),
            pltpu.VMEM((2 * NZ, VIEWS * NZ), BF16),
            pltpu.VMEM((2 * NZ, 2 * NZ), BF16),
            pltpu.VMEM((2 * NZ, 2 * NZ), BF16),
            pltpu.VMEM((2 * ITERS, NZ, NZ), F32),
            pltpu.VMEM((2 * NZ, 2 * NZ), F32),
            pltpu.VMEM((1, 1, 128), F32),
            pltpu.VMEM((4, 1, 128), F32),
            pltpu.VMEM((TILES, 1, 128), F32),
            pltpu.VMEM((1, 1, 128), F32),
            dma((4,)),
            dma((DEPTHS,)),
            dma((2 * CHUNKS,)),
            dma((CHUNKS,)),
            dma((CHUNKS,)),
            dma((CHUNKS,)),
            dma((CHUNKS,)),
            dma((3,)),
            dma((3,)),
            dma((1,)),
            dma((1,)),
        ],
        compiler_params=pltpu.CompilerParams(
            collective_id=0, has_side_effects=True, vmem_limit_bytes=48 << 20
        ),
        name="solve",
    )(
        init,
        measured.reshape(VIEWS * NZ, XT, YD),
        pltpu.with_memory_space_constraint(mask.T, pltpu.HBM),
        pltpu.with_memory_space_constraint(
            kernel_index.reshape(VIEWS * ZBANDS, TILES), pltpu.HBM
        ),
        pltpu.with_memory_space_constraint(kernels, pltpu.HBM),
    )
    return pl.pallas_call(
        place_kernel,
        out_shape=jax.ShapeDtypeStruct((DEPTHS, nx, 128), F32),
        in_specs=[vmem],
        out_specs=hbm,
        scratch_shapes=[dma((4 * DEPTHS,))],
        compiler_params=pltpu.CompilerParams(vmem_limit_bytes=8 << 20),
        name="place",
    )(solved)


def solution(mesh):
    return jax.shard_map(
        local,
        mesh=mesh,
        in_specs=(P("gz", None, "gy"), P(None, None, "gz", "gy"), P(), P(), P()),
        out_specs=P("gz", None, "gy"),
        check_vma=False,
    )
```

```python
import jax
import jax.numpy as jnp
from jax import lax
from jax.experimental import pallas as pl
from jax.experimental.pallas import tpu as pltpu
from jax.sharding import PartitionSpec as P

NZ = 128
XT = 64
YD = 128
ZBW = 16
TAPS = 31
VIEWS = 4
NK = 16
ITERS = 4
HALF = 15
ZBANDS = 8
NY_BLOCKS = 8
TILES = 32
RINGX, RINGY, CORES = 4, 4, 2
DEPTHS = 4
CHUNKS = 4
ROWS = 8
PIECE = DEPTHS * ROWS
PART = TILES * PIECE

MESH = pl.DeviceIdType.MESH
HIGHEST = lax.Precision.HIGHEST
F32 = jnp.float32
BF16 = jnp.bfloat16


def away(d, n):
    return min(d, n - d)


OFFSETS = sorted(
    ((dx, dy, dc) for dx in range(RINGX) for dy in range(RINGY) for dc in range(CORES)),
    key=lambda t: (-(away(t[0], RINGX) + away(t[1], RINGY)), t),
)
OFFSETS.remove((0, 0, 0))
FAR = len(OFFSETS)


def dot(a, b, precision=None):
    return jnp.dot(a, b, precision=precision, preferred_element_type=F32)


def dot_nt(a, b):
    return lax.dot_general(
        a, b, (((1,), (1,)), ((), ())), precision=HIGHEST, preferred_element_type=F32
    )


def halves(value):
    high = value.astype(BF16)
    return high, (value - high.astype(F32)).astype(BF16)


def put_ops(ops, matrix):
    high, low = halves(matrix)
    ops[0:NZ, 0:NZ] = high
    ops[0:NZ, NZ:] = high
    ops[NZ:, 0:NZ] = low
    ops[NZ:, NZ:] = jnp.zeros((NZ, NZ), BF16)


def pack(low_rows, high_rows, upper, lane):
    rolled = pltpu.roll(jnp.where(upper, low_rows, high_rows), 64, 1)
    return jnp.where(
        lane < 64, jnp.where(upper, rolled, low_rows), jnp.where(upper, high_rows, rolled)
    )


def mix(row, low_rows, high_rows, upper, lane):
    rolled = pltpu.roll(row, 64, 1)
    left = lane < 64
    spread_low = jnp.where(upper, rolled, row)
    spread_high = jnp.where(upper, row, rolled)
    tissue = jnp.logical_xor(left, upper)
    return jnp.where(tissue, spread_low, low_rows), jnp.where(tissue, spread_high, high_rows)


def cg_weights(moments, centre, half):
    product = [
        [0.5 * (moments[i + j] + moments[abs(i - j)]) for j in range(ITERS + 1)]
        for i in range(ITERS)
    ]

    def apply(a):
        out = [centre * value for value in a] + [None]

        def put(j, value):
            out[j] = value if out[j] is None else out[j] + value

        for j, value in enumerate(a):
            if j == 0:
                put(1, half * value)
            else:
                put(j + 1, 0.5 * half * value)
                put(j - 1, 0.5 * half * value)
        return out

    def square(a):
        total = None
        for i in range(len(a)):
            row = a[i] * product[i][i]
            for j in range(i + 1, len(a)):
                row = row + 2.0 * a[j] * product[i][j]
            total = a[i] * row if total is None else total + a[i] * row
        return total

    def inner(a, b):
        total = None
        for i in range(len(a)):
            row = None
            for j in range(len(b)):
                term = b[j] * product[i][j]
                row = term if row is None else row + term
            total = a[i] * row if total is None else total + a[i] * row
        return total

    one = jnp.ones_like(moments[0])
    residual, direction, step = [one], [one], []
    norm_now = moments[0]
    for iteration in range(ITERS):
        image = apply(direction)
        alpha = norm_now / inner(direction, image)
        step = [
            alpha * d if j >= len(step) else step[j] + alpha * d for j, d in enumerate(direction)
        ]
        if iteration == ITERS - 1:
            return step
        residual = [
            -alpha * v if j >= len(residual) else residual[j] - alpha * v
            for j, v in enumerate(image)
        ]
        norm_next = square(residual)
        ratio = norm_next / norm_now
        direction = [
            r if j >= len(direction) else r + ratio * direction[j] for j, r in enumerate(residual)
        ]
        norm_now = norm_next


def solve_kernel(
    init_ref, measured_ref, mask_hbm, index_hbm, kernels_hbm, prior,
    mask_ref, index_ref, index_row_ref, kernels_ref, views, sent, field, back, solved, resid, stacks, taps, kpad, blur_rows, blur_ops, gram_ops, step_ops, cheb_ops, early,
    cheb, total, part, part_z, part_g, sum_z,
    small_sem, prior_sem, view_sem, send_sem, recv_sem, back_sem, ret_sem, z_send, z_recv, g_send, g_recv,
):
    me = lax.axis_index("gz")
    row = lax.axis_index("gy")
    my_core = lax.rem(me, CORES)
    my_x = lax.rem(lax.div(me, CORES), RINGX)
    my_y = lax.div(me, CORES * RINGX)

    def peer(offset):
        dx, dy, dc = offset
        return (
            lax.rem(my_y + dy, RINGY) * RINGX + lax.rem(my_x + dx, RINGX)
        ) * CORES + lax.rem(my_core + dc, CORES)

    def prior_copy(d):
        return pltpu.make_async_copy(init_ref.at[d], prior.at[d], prior_sem.at[d])

    def view_copy(i):
        return pltpu.make_async_copy(
            measured_ref.at[:, pl.ds(i * ROWS, ROWS), :], views.at[i], view_sem.at[i]
        )

    small = [
        pltpu.make_async_copy(source, target, small_sem.at[i])
        for i, (source, target) in enumerate(
            (
                (mask_hbm, mask_ref),
                (index_hbm, index_ref),
                (index_hbm, index_row_ref),
                (kernels_hbm, kernels_ref),
            )
        )
    ]
    for copy in small[:1]:
        copy.start()
    for d in range(DEPTHS):
        prior_copy(d).start()
    for copy in small[1:]:
        copy.start()

    barrier = pltpu.get_barrier_semaphore()
    for offset in OFFSETS:
        pl.semaphore_signal(barrier, inc=1, device_id=(peer(offset), row), device_id_type=MESH)
    for dz in range(1, 4):
        pl.semaphore_signal(
            barrier, inc=1, device_id=(me, lax.rem(row + dz, 4)), device_id_type=MESH
        )

    lane8 = lax.broadcasted_iota(jnp.int32, (ROWS, 128), 1)
    for copy in small:
        copy.wait()
    for d in range(DEPTHS):
        prior_copy(d).wait()
    for c in range(CHUNKS):
        for i in (c, c + CHUNKS):
            view_copy(i).start()

    def pack_chunk(c):
        @pl.loop(0, TILES)
        def _(p):
            upper = jnp.full((ROWS, 128), mask_ref[2 * row + 1, p], jnp.int32) != 0
            for d in range(DEPTHS):
                low = pl.multiple_of(p * XT + c * ROWS, ROWS)
                high = pl.multiple_of(p * XT + c * ROWS + XT // 2, ROWS)
                packed = pack(
                    prior[d, pl.ds(low, ROWS), :], prior[d, pl.ds(high, ROWS), :], upper, lane8
                )
                sent[c, pl.ds(pl.multiple_of(p * PIECE + d * ROWS, ROWS), ROWS), :] = packed

    def send_chunk(source, target, c, send, recv):
        for offset in OFFSETS:
            p = peer(offset)
            pltpu.make_async_remote_copy(
                src_ref=source.at[c, pl.ds(pl.multiple_of(p * PIECE, PIECE), PIECE)],
                dst_ref=target.at[c, pl.ds(pl.multiple_of(me * PIECE, PIECE), PIECE)],
                send_sem=send.at[c],
                recv_sem=recv.at[c],
                device_id=(p, row),
                device_id_type=MESH,
            ).start()

    def chunk_copy(source, target, c, send, recv):
        return pltpu.make_async_remote_copy(
            src_ref=source.at[c, pl.ds(0, FAR * PIECE)],
            dst_ref=target.at[c, pl.ds(0, FAR * PIECE)],
            send_sem=send.at[c],
            recv_sem=recv.at[c],
            device_id=(peer(OFFSETS[0]), row),
            device_id_type=MESH,
        )

    pack_chunk(0)
    pl.semaphore_wait(barrier, FAR + 3)

    @pl.loop(0, CHUNKS)
    def _(c):
        send_chunk(sent, field, c, send_sem, recv_sem)

        @pl.when(c < CHUNKS - 1)
        def _():
            pack_chunk(c + 1)

    own = pl.ds(pl.multiple_of(me * PIECE, PIECE), PIECE)
    for c in range(CHUNKS):
        field[c, own, :] = sent[c, own, :]

    lane = lax.broadcasted_iota(jnp.int32, (NZ, NZ), 1)
    depth = lax.broadcasted_iota(jnp.int32, (NZ, NZ), 0)
    kpad[...] = jnp.zeros((NK, 128), F32)
    kpad[:, 0:TAPS] = kernels_ref[...]
    for v in range(VIEWS):
        for band in range(ZBANDS):
            k = index_ref[v * ZBANDS + band, me]
            taps[pl.ds((v * ZBANDS + band) * ZBW, ZBW), :] = jnp.broadcast_to(
                kpad[pl.ds(k, 1), :], (ZBW, 128)
            )
    near = jnp.abs(lane - depth) <= HALF
    for v in range(VIEWS):
        at = pl.ds(v * NZ, NZ)
        mat = jnp.where(
            near, pltpu.roll(taps[at, :], 128 - HALF, 1, stride=1, stride_axis=0), 0.0
        )
        turned = mat.T
        blur_rows[at, :] = mat
        high, low = halves(turned)
        blur_ops[0:NZ, at] = high
        blur_ops[NZ:, at] = low
        taps[at, :] = turned
    grams = dot(taps[0:NZ, :], blur_rows[0:NZ, :], HIGHEST)
    for v in range(1, VIEWS):
        at = pl.ds(v * NZ, NZ)
        grams = grams + dot(taps[at, :], blur_rows[at, :], HIGHEST)
    put_ops(gram_ops, grams)

    bins = lax.broadcasted_iota(jnp.int32, (NK, TILES), 0)
    span = lax.broadcasted_iota(jnp.int32, (3 * ZBW, 128), 0)
    tap = lax.broadcasted_iota(jnp.int32, (3 * ZBW, 128), 1)
    window = jnp.where(jnp.logical_and(tap >= span - ZBW, tap < span), 1.0, 0.0)
    sums = dot_nt(window, kpad[...]) * dot_nt(jnp.ones((3 * ZBW, 128), F32), kpad[...])
    spreads = []
    for band in range(ZBANDS):
        counts = jnp.zeros((NK, TILES), F32)
        for v in range(VIEWS):
            at = v * ZBANDS + band
            counts = counts + jnp.where(index_row_ref[at : at + 1, :] == bins, 1.0, 0.0)
        spreads.append(dot(sums, counts, HIGHEST))
    row_sums = None
    for band in range(ZBANDS):
        here = spreads[band][ZBW : 2 * ZBW, :]
        if band > 0:
            here = here + spreads[band - 1][2 * ZBW :, :]
        if band < ZBANDS - 1:
            here = here + spreads[band + 1][0:ZBW, :]
        row_sums = here if row_sums is None else jnp.maximum(row_sums, here)
    bound = jnp.max(jnp.max(row_sums, axis=0, keepdims=True), axis=1, keepdims=True)
    half = jnp.broadcast_to(0.5001 * bound, (1, 128))
    centre = 1.0 + half

    eye = jnp.where(lane == depth, 1.0, 0.0)
    cheb[0] = eye
    cheb[1] = grams / half - eye
    cheb[2] = 2.0 * dot(cheb[1], cheb[1], HIGHEST) - eye
    cheb[3] = 2.0 * dot(cheb[1], cheb[2], HIGHEST) - cheb[1]
    cheb[4] = 2.0 * dot(cheb[2], cheb[2], HIGHEST) - eye
    cheb[5] = 2.0 * dot(cheb[2], cheb[3], HIGHEST) - cheb[1]
    cheb[6] = 2.0 * dot(cheb[3], cheb[3], HIGHEST) - eye
    cheb[7] = 2.0 * dot(cheb[3], cheb[4], HIGHEST) - cheb[1]
    for j in range(1, ITERS):
        put_ops(cheb_ops.at[j - 1], cheb[j])

    mine = jnp.full((NZ, 128), mask_ref[2 * row + 1, me], jnp.int32) != 0

    for i in range(2 * CHUNKS):
        view_copy(i).wait()

    @pl.loop(0, CHUNKS)
    def _(c):
        @pl.loop(0, ROWS // 2)
        def _(pair):
            product = None
            for v in range(VIEWS):
                sides = []
                for r in range(2):
                    at = pl.ds(pair * 2 + r, NZ, stride=ROWS)
                    lows = views.at[c, pl.ds(v * NZ, NZ)].reshape(NZ * ROWS, 128)[at, :]
                    highs = views.at[c + CHUNKS, pl.ds(v * NZ, NZ)].reshape(NZ * ROWS, 128)[at, :]
                    sides.append(pack(lows, highs, mine, lane))
                high, low = halves(jnp.concatenate(sides, axis=1))
                ops = blur_ops[:, pl.ds(v * NZ, NZ)]
                both = dot(ops, high)
                term = both[0:NZ] + both[NZ:] + dot(ops[0:NZ], low)
                product = term if product is None else product + term
            resid[c * (ROWS // 2) + pair] = product

    def columns(c, pair):
        sides = [field[c, pl.ds(pair * 2 + r, NZ, stride=ROWS), :] for r in range(2)]
        return jnp.concatenate(sides, axis=1)

    def stacked(value):
        return jnp.concatenate(halves(value), axis=0)

    def times(ops, stack):
        both = dot(ops[...], stack)
        return both[0:NZ] + both[NZ:]

    total[...] = jnp.zeros((2 * NZ, 2 * NZ), F32)

    @pl.loop(0, CHUNKS)
    def _(c):
        chunk_copy(sent, field, c, send_sem, recv_sem).wait_recv()

        @pl.loop(0, ROWS // 2)
        def _(pair):
            at = c * (ROWS // 2) + pair
            first = resid[at] - times(gram_ops, stacked(columns(c, pair)))
            stack = stacked(first)
            stacks[at] = stack
            resid[at] = first
            total[...] += lax.dot_general(
                stack, stack, (((1,), (1,)), ((), ())), preferred_element_type=F32
            )

    lane1 = lax.broadcasted_iota(jnp.int32, (1, 128), 1)
    local = jnp.zeros((1, 128), F32)
    square = total[0:NZ, 0:NZ] + (total[0:NZ, NZ:] + total[NZ:, 0:NZ]) + total[NZ:, NZ:]
    for k in range(2 * ITERS):
        value = jnp.sum(cheb[k] * square, axis=0, keepdims=True)
        local = jnp.where(lane1 == k, jnp.sum(value, axis=1, keepdims=True), local)
    part[0] = local
    part_z[row] = local
    hops = []
    for dz in range(1, 4):
        copy = pltpu.make_async_remote_copy(
            src_ref=part.at[0],
            dst_ref=part_z.at[row],
            send_sem=z_send.at[dz - 1],
            recv_sem=z_recv.at[dz - 1],
            device_id=(me, lax.rem(row + dz, 4)),
            device_id_type=MESH,
        )
        copy.start()
        hops.append(copy)

    @pl.loop(0, ROWS // 2)
    def _(pair):
        for j in range(ITERS - 1):
            early[j, pair] = times(cheb_ops.at[j], stacks[pair])

    for copy in hops:
        copy.wait()
    along = (part_z[0] + part_z[1]) + (part_z[2] + part_z[3])
    sum_z[0] = along
    part_g[me] = along
    for offset in OFFSETS:
        p = peer(offset)
        pltpu.make_async_remote_copy(
            src_ref=sum_z.at[0],
            dst_ref=part_g.at[me],
            send_sem=g_send.at[0],
            recv_sem=g_recv.at[0],
            device_id=(p, row),
            device_id_type=MESH,
        ).start()
    everyone = pltpu.make_async_remote_copy(
        src_ref=part_g.at[pl.ds(0, FAR)],
        dst_ref=part_g.at[pl.ds(0, FAR)],
        send_sem=g_send.at[0],
        recv_sem=g_recv.at[0],
        device_id=(peer(OFFSETS[0]), row),
        device_id_type=MESH,
    )
    everyone.wait_recv()
    whole = jnp.sum(part_g[...], axis=0)
    moments = [
        jnp.broadcast_to(
            jnp.sum(jnp.where(lane1 == k, whole, 0.0), axis=1, keepdims=True), (1, 128)
        )
        for k in range(2 * ITERS)
    ]
    weights = cg_weights(moments, centre, half)

    def put_back(c, pair, step):
        moved = columns(c, pair) + step
        for r in range(2):
            back[c, pl.ds(pair * 2 + r, NZ, stride=ROWS), :] = moved[:, r * 128 : (r + 1) * 128]

    def send_back(c):
        solved[c, own, :] = back[c, own, :]
        send_chunk(back, solved, c, back_sem, ret_sem)

    wide = [jnp.concatenate([weight, weight], axis=1) for weight in weights]

    @pl.loop(0, ROWS // 2)
    def _(pair):
        step = wide[0] * resid[pair]
        for j in range(1, ITERS):
            step = step + wide[j] * early[j - 1, pair]
        put_back(0, pair, step)

    send_back(0)
    poly = weights[0] * cheb[0]
    for j in range(1, ITERS):
        poly = poly + weights[j] * cheb[j]
    put_ops(step_ops, poly)

    @pl.loop(1, CHUNKS)
    def _(c):
        @pl.loop(0, ROWS // 2)
        def _(pair):
            put_back(c, pair, times(step_ops, stacks[c * (ROWS // 2) + pair]))

        send_back(c)

    @pl.loop(0, CHUNKS)
    def _(c):
        chunk_copy(back, solved, c, back_sem, ret_sem).wait_recv()

        @pl.loop(0, TILES)
        def _(b):
            upper = jnp.full((ROWS, 128), mask_ref[2 * row + 1, b], jnp.int32) != 0
            for d in range(DEPTHS):
                low = pl.ds(pl.multiple_of(b * XT + c * ROWS, ROWS), ROWS)
                high = pl.ds(pl.multiple_of(b * XT + c * ROWS + XT // 2, ROWS), ROWS)
                prior[d, low, :], prior[d, high, :] = mix(
                    solved[c, pl.ds(pl.multiple_of(b * PIECE + d * ROWS, ROWS), ROWS), :],
                    prior[d, low, :], prior[d, high, :], upper, lane8,
                )

    everyone.wait_send()
    for c in range(CHUNKS):
        chunk_copy(sent, field, c, send_sem, recv_sem).wait_send()
        chunk_copy(back, solved, c, back_sem, ret_sem).wait_send()


def place_kernel(solved_ref, out_ref, sem):
    part = TILES * XT // 4
    copies = [
        pltpu.make_async_copy(
            solved_ref.at[d, pl.ds(i * part, part)],
            out_ref.at[d, pl.ds(i * part, part)],
            sem.at[d * 4 + i],
        )
        for d in range(DEPTHS)
        for i in range(4)
    ]
    for copy in copies:
        copy.start()
    for copy in copies:
        copy.wait()


def local(init, measured, mask, kernel_index, kernels):
    nx = TILES * XT
    vmem = pl.BlockSpec(memory_space=pltpu.VMEM)
    hbm = pl.BlockSpec(memory_space=pltpu.HBM)
    dma = pltpu.SemaphoreType.DMA
    solved = pl.pallas_call(
        solve_kernel,
        out_shape=jax.ShapeDtypeStruct((DEPTHS, nx, 128), F32),
        in_specs=[hbm] * 5,
        out_specs=vmem,
        scratch_shapes=[
            pltpu.SMEM((NY_BLOCKS, TILES), jnp.int32),
            pltpu.SMEM((VIEWS * ZBANDS, TILES), jnp.int32),
            pltpu.VMEM((VIEWS * ZBANDS, TILES), jnp.int32),
            pltpu.VMEM((NK, TAPS), F32),
            pltpu.VMEM((2 * CHUNKS, VIEWS * NZ, ROWS, 128), F32),
            pltpu.VMEM((CHUNKS, PART, 128), F32),
            pltpu.VMEM((CHUNKS, PART, 128), F32),
            pltpu.VMEM((CHUNKS, PART, 128), F32),
            pltpu.VMEM((CHUNKS, PART, 128), F32),
            pltpu.VMEM((CHUNKS * ROWS // 2, NZ, 256), F32),
            pltpu.VMEM((CHUNKS * ROWS // 2, 2 * NZ, 256), BF16),
            pltpu.VMEM((VIEWS * NZ, 128), F32),
            pltpu.VMEM((NK, 128), F32),
            pltpu.VMEM((VIEWS * NZ, NZ), F32),
            pltpu.VMEM((2 * NZ, VIEWS * NZ), BF16),
            pltpu.VMEM((2 * NZ, 2 * NZ), BF16),
            pltpu.VMEM((2 * NZ, 2 * NZ), BF16),
            pltpu.VMEM((ITERS - 1, 2 * NZ, 2 * NZ), BF16),
            pltpu.VMEM((ITERS - 1, ROWS // 2, NZ, 256), F32),
            pltpu.VMEM((2 * ITERS, NZ, NZ), F32),
            pltpu.VMEM((2 * NZ, 2 * NZ), F32),
            pltpu.VMEM((1, 1, 128), F32),
            pltpu.VMEM((4, 1, 128), F32),
            pltpu.VMEM((TILES, 1, 128), F32),
            pltpu.VMEM((1, 1, 128), F32),
            dma((4,)),
            dma((DEPTHS,)),
            dma((2 * CHUNKS,)),
            dma((CHUNKS,)),
            dma((CHUNKS,)),
            dma((CHUNKS,)),
            dma((CHUNKS,)),
            dma((3,)),
            dma((3,)),
            dma((1,)),
            dma((1,)),
        ],
        compiler_params=pltpu.CompilerParams(
            collective_id=0, has_side_effects=True, vmem_limit_bytes=48 << 20
        ),
        name="solve",
    )(
        init,
        measured.reshape(VIEWS * NZ, XT, YD),
        pltpu.with_memory_space_constraint(mask.T, pltpu.HBM),
        pltpu.with_memory_space_constraint(
            kernel_index.reshape(VIEWS * ZBANDS, TILES), pltpu.HBM
        ),
        pltpu.with_memory_space_constraint(kernels, pltpu.HBM),
    )
    return pl.pallas_call(
        place_kernel,
        out_shape=jax.ShapeDtypeStruct((DEPTHS, nx, 128), F32),
        in_specs=[vmem],
        out_specs=hbm,
        scratch_shapes=[dma((4 * DEPTHS,))],
        compiler_params=pltpu.CompilerParams(vmem_limit_bytes=8 << 20),
        name="place",
    )(solved)


def solution(mesh):
    return jax.shard_map(
        local,
        mesh=mesh,
        in_specs=(P("gz", None, "gy"), P(None, None, "gz", "gy"), P(), P(), P()),
        out_specs=P("gz", None, "gy"),
        check_vma=False,
    )
```

```python
import jax
import jax.numpy as jnp
from jax import lax
from jax.experimental import pallas as pl
from jax.experimental.pallas import tpu as pltpu
from jax.sharding import PartitionSpec as P

NZ = 128
XT = 64
YD = 128
ZBW = 16
TAPS = 31
VIEWS = 4
NK = 16
ITERS = 4
HALF = 15
ZBANDS = 8
NY_BLOCKS = 8
TILES = 32
RINGX, RINGY, CORES = 4, 4, 2
DEPTHS = 4
CHUNKS = 4
ROWS = 8
PIECE = DEPTHS * ROWS
PART = TILES * PIECE

MESH = pl.DeviceIdType.MESH
HIGHEST = lax.Precision.HIGHEST
F32 = jnp.float32
BF16 = jnp.bfloat16


def away(d, n):
    return min(d, n - d)


OFFSETS = sorted(
    ((dx, dy, dc) for dx in range(RINGX) for dy in range(RINGY) for dc in range(CORES)),
    key=lambda t: (-(away(t[0], RINGX) + away(t[1], RINGY)), t),
)
OFFSETS.remove((0, 0, 0))
FAR = len(OFFSETS)


def dot(a, b, precision=None):
    return jnp.dot(a, b, precision=precision, preferred_element_type=F32)


def dot_nt(a, b):
    return lax.dot_general(
        a, b, (((1,), (1,)), ((), ())), precision=HIGHEST, preferred_element_type=F32
    )


def halves(value):
    high = value.astype(BF16)
    return high, (value - high.astype(F32)).astype(BF16)


def put_ops(ops, matrix):
    high, low = halves(matrix)
    ops[0:NZ, 0:NZ] = high
    ops[0:NZ, NZ:] = high
    ops[NZ:, 0:NZ] = low
    ops[NZ:, NZ:] = jnp.zeros((NZ, NZ), BF16)


def pack(low_rows, high_rows, upper, lane):
    rolled = pltpu.roll(jnp.where(upper, low_rows, high_rows), 64, 1)
    return jnp.where(
        lane < 64, jnp.where(upper, rolled, low_rows), jnp.where(upper, high_rows, rolled)
    )


def mix(row, low_rows, high_rows, upper, lane):
    rolled = pltpu.roll(row, 64, 1)
    left = lane < 64
    spread_low = jnp.where(upper, rolled, row)
    spread_high = jnp.where(upper, row, rolled)
    tissue = jnp.logical_xor(left, upper)
    return jnp.where(tissue, spread_low, low_rows), jnp.where(tissue, spread_high, high_rows)


def cg_weights(moments, centre, half):
    product = [
        [0.5 * (moments[i + j] + moments[abs(i - j)]) for j in range(ITERS + 1)]
        for i in range(ITERS)
    ]

    def apply(a):
        out = [centre * value for value in a] + [None]

        def put(j, value):
            out[j] = value if out[j] is None else out[j] + value

        for j, value in enumerate(a):
            if j == 0:
                put(1, half * value)
            else:
                put(j + 1, 0.5 * half * value)
                put(j - 1, 0.5 * half * value)
        return out

    def square(a):
        total = None
        for i in range(len(a)):
            row = a[i] * product[i][i]
            for j in range(i + 1, len(a)):
                row = row + 2.0 * a[j] * product[i][j]
            total = a[i] * row if total is None else total + a[i] * row
        return total

    def inner(a, b):
        total = None
        for i in range(len(a)):
            row = None
            for j in range(len(b)):
                term = b[j] * product[i][j]
                row = term if row is None else row + term
            total = a[i] * row if total is None else total + a[i] * row
        return total

    one = jnp.ones_like(moments[0])
    residual, direction, step = [one], [one], []
    norm_now = moments[0]
    for iteration in range(ITERS):
        image = apply(direction)
        alpha = norm_now / inner(direction, image)
        step = [
            alpha * d if j >= len(step) else step[j] + alpha * d for j, d in enumerate(direction)
        ]
        if iteration == ITERS - 1:
            return step
        residual = [
            -alpha * v if j >= len(residual) else residual[j] - alpha * v
            for j, v in enumerate(image)
        ]
        norm_next = square(residual)
        ratio = norm_next / norm_now
        direction = [
            r if j >= len(direction) else r + ratio * direction[j] for j, r in enumerate(residual)
        ]
        norm_now = norm_next


def solve_kernel(
    init_ref, measured_ref, mask_hbm, index_hbm, kernels_hbm, prior,
    mask_ref, index_ref, index_row_ref, kernels_ref, views, sent, field, back, solved, resid, stacks, taps, kpad, blur_rows, blur_ops, gram_ops, step_ops, cheb_ops, early,
    cheb, total, part, part_z, part_g, sum_z,
    small_sem, prior_sem, view_sem, send_sem, recv_sem, back_sem, ret_sem, z_send, z_recv, g_send, g_recv,
):
    me = lax.axis_index("gz")
    row = lax.axis_index("gy")
    my_core = lax.rem(me, CORES)
    my_x = lax.rem(lax.div(me, CORES), RINGX)
    my_y = lax.div(me, CORES * RINGX)

    def peer(offset):
        dx, dy, dc = offset
        sign = 1 - 2 * my_core
        dx, dy = dx * sign + RINGX, dy * sign + RINGY
        return (
            lax.rem(my_y + dy, RINGY) * RINGX + lax.rem(my_x + dx, RINGX)
        ) * CORES + lax.rem(my_core + dc, CORES)

    def prior_copy(d):
        return pltpu.make_async_copy(init_ref.at[d], prior.at[d], prior_sem.at[d])

    def view_copy(i):
        return pltpu.make_async_copy(
            measured_ref.at[:, pl.ds(i * ROWS, ROWS), :], views.at[i], view_sem.at[i]
        )

    small = [
        pltpu.make_async_copy(source, target, small_sem.at[i])
        for i, (source, target) in enumerate(
            (
                (mask_hbm, mask_ref),
                (index_hbm, index_ref),
                (index_hbm, index_row_ref),
                (kernels_hbm, kernels_ref),
            )
        )
    ]
    for copy in small[:1]:
        copy.start()
    for d in range(DEPTHS):
        prior_copy(d).start()
    for copy in small[1:]:
        copy.start()

    barrier = pltpu.get_barrier_semaphore()
    for offset in OFFSETS:
        pl.semaphore_signal(barrier, inc=1, device_id=(peer(offset), row), device_id_type=MESH)
    for dz in range(1, 4):
        pl.semaphore_signal(
            barrier, inc=1, device_id=(me, lax.rem(row + dz, 4)), device_id_type=MESH
        )

    lane8 = lax.broadcasted_iota(jnp.int32, (ROWS, 128), 1)
    for copy in small:
        copy.wait()
    for d in range(DEPTHS):
        prior_copy(d).wait()
    for c in range(CHUNKS):
        for i in (c, c + CHUNKS):
            view_copy(i).start()

    def pack_chunk(c):
        @pl.loop(0, TILES)
        def _(p):
            upper = jnp.full((ROWS, 128), mask_ref[2 * row + 1, p], jnp.int32) != 0
            for d in range(DEPTHS):
                low = pl.multiple_of(p * XT + c * ROWS, ROWS)
                high = pl.multiple_of(p * XT + c * ROWS + XT // 2, ROWS)
                packed = pack(
                    prior[d, pl.ds(low, ROWS), :], prior[d, pl.ds(high, ROWS), :], upper, lane8
                )
                sent[c, pl.ds(pl.multiple_of(p * PIECE + d * ROWS, ROWS), ROWS), :] = packed

    def send_chunk(source, target, c, send, recv):
        for offset in OFFSETS:
            p = peer(offset)
            pltpu.make_async_remote_copy(
                src_ref=source.at[c, pl.ds(pl.multiple_of(p * PIECE, PIECE), PIECE)],
                dst_ref=target.at[c, pl.ds(pl.multiple_of(me * PIECE, PIECE), PIECE)],
                send_sem=send.at[c],
                recv_sem=recv.at[c],
                device_id=(p, row),
                device_id_type=MESH,
            ).start()

    def chunk_copy(source, target, c, send, recv):
        return pltpu.make_async_remote_copy(
            src_ref=source.at[c, pl.ds(0, FAR * PIECE)],
            dst_ref=target.at[c, pl.ds(0, FAR * PIECE)],
            send_sem=send.at[c],
            recv_sem=recv.at[c],
            device_id=(peer(OFFSETS[0]), row),
            device_id_type=MESH,
        )

    pack_chunk(0)
    pl.semaphore_wait(barrier, FAR + 3)

    @pl.loop(0, CHUNKS)
    def _(c):
        send_chunk(sent, field, c, send_sem, recv_sem)

        @pl.when(c < CHUNKS - 1)
        def _():
            pack_chunk(c + 1)

    own = pl.ds(pl.multiple_of(me * PIECE, PIECE), PIECE)
    for c in range(CHUNKS):
        field[c, own, :] = sent[c, own, :]

    lane = lax.broadcasted_iota(jnp.int32, (NZ, NZ), 1)
    depth = lax.broadcasted_iota(jnp.int32, (NZ, NZ), 0)
    kpad[...] = jnp.zeros((NK, 128), F32)
    kpad[:, 0:TAPS] = kernels_ref[...]
    for v in range(VIEWS):
        for band in range(ZBANDS):
            k = index_ref[v * ZBANDS + band, me]
            taps[pl.ds((v * ZBANDS + band) * ZBW, ZBW), :] = jnp.broadcast_to(
                kpad[pl.ds(k, 1), :], (ZBW, 128)
            )
    near = jnp.abs(lane - depth) <= HALF
    for v in range(VIEWS):
        at = pl.ds(v * NZ, NZ)
        mat = jnp.where(
            near, pltpu.roll(taps[at, :], 128 - HALF, 1, stride=1, stride_axis=0), 0.0
        )
        turned = mat.T
        blur_rows[at, :] = mat
        high, low = halves(turned)
        blur_ops[0:NZ, at] = high
        blur_ops[NZ:, at] = low
        taps[at, :] = turned
    grams = dot(taps[0:NZ, :], blur_rows[0:NZ, :], HIGHEST)
    for v in range(1, VIEWS):
        at = pl.ds(v * NZ, NZ)
        grams = grams + dot(taps[at, :], blur_rows[at, :], HIGHEST)
    put_ops(gram_ops, grams)

    bins = lax.broadcasted_iota(jnp.int32, (NK, TILES), 0)
    span = lax.broadcasted_iota(jnp.int32, (3 * ZBW, 128), 0)
    tap = lax.broadcasted_iota(jnp.int32, (3 * ZBW, 128), 1)
    window = jnp.where(jnp.logical_and(tap >= span - ZBW, tap < span), 1.0, 0.0)
    sums = dot_nt(window, kpad[...]) * dot_nt(jnp.ones((3 * ZBW, 128), F32), kpad[...])
    spreads = []
    for band in range(ZBANDS):
        counts = jnp.zeros((NK, TILES), F32)
        for v in range(VIEWS):
            at = v * ZBANDS + band
            counts = counts + jnp.where(index_row_ref[at : at + 1, :] == bins, 1.0, 0.0)
        spreads.append(dot(sums, counts, HIGHEST))
    row_sums = None
    for band in range(ZBANDS):
        here = spreads[band][ZBW : 2 * ZBW, :]
        if band > 0:
            here = here + spreads[band - 1][2 * ZBW :, :]
        if band < ZBANDS - 1:
            here = here + spreads[band + 1][0:ZBW, :]
        row_sums = here if row_sums is None else jnp.maximum(row_sums, here)
    bound = jnp.max(jnp.max(row_sums, axis=0, keepdims=True), axis=1, keepdims=True)
    half = jnp.broadcast_to(0.5001 * bound, (1, 128))
    centre = 1.0 + half

    eye = jnp.where(lane == depth, 1.0, 0.0)
    cheb[0] = eye
    cheb[1] = grams / half - eye
    cheb[2] = 2.0 * dot(cheb[1], cheb[1], HIGHEST) - eye
    cheb[3] = 2.0 * dot(cheb[1], cheb[2], HIGHEST) - cheb[1]
    cheb[4] = 2.0 * dot(cheb[2], cheb[2], HIGHEST) - eye
    cheb[5] = 2.0 * dot(cheb[2], cheb[3], HIGHEST) - cheb[1]
    cheb[6] = 2.0 * dot(cheb[3], cheb[3], HIGHEST) - eye
    cheb[7] = 2.0 * dot(cheb[3], cheb[4], HIGHEST) - cheb[1]
    for j in range(1, ITERS):
        put_ops(cheb_ops.at[j - 1], cheb[j])

    mine = jnp.full((NZ, 128), mask_ref[2 * row + 1, me], jnp.int32) != 0

    for i in range(2 * CHUNKS):
        view_copy(i).wait()

    @pl.loop(0, CHUNKS)
    def _(c):
        @pl.loop(0, ROWS // 2)
        def _(pair):
            product = None
            for v in range(VIEWS):
                sides = []
                for r in range(2):
                    at = pl.ds(pair * 2 + r, NZ, stride=ROWS)
                    lows = views.at[c, pl.ds(v * NZ, NZ)].reshape(NZ * ROWS, 128)[at, :]
                    highs = views.at[c + CHUNKS, pl.ds(v * NZ, NZ)].reshape(NZ * ROWS, 128)[at, :]
                    sides.append(pack(lows, highs, mine, lane))
                high, low = halves(jnp.concatenate(sides, axis=1))
                ops = blur_ops[:, pl.ds(v * NZ, NZ)]
                both = dot(ops, high)
                term = both[0:NZ] + both[NZ:] + dot(ops[0:NZ], low)
                product = term if product is None else product + term
            resid[c * (ROWS // 2) + pair] = product

    def columns(c, pair):
        sides = [field[c, pl.ds(pair * 2 + r, NZ, stride=ROWS), :] for r in range(2)]
        return jnp.concatenate(sides, axis=1)

    def stacked(value):
        return jnp.concatenate(halves(value), axis=0)

    def times(ops, stack):
        both = dot(ops[...], stack)
        return both[0:NZ] + both[NZ:]

    total[...] = jnp.zeros((2 * NZ, 2 * NZ), F32)

    @pl.loop(0, CHUNKS)
    def _(c):
        chunk_copy(sent, field, c, send_sem, recv_sem).wait_recv()

        @pl.loop(0, ROWS // 2)
        def _(pair):
            at = c * (ROWS // 2) + pair
            first = resid[at] - times(gram_ops, stacked(columns(c, pair)))
            stack = stacked(first)
            stacks[at] = stack
            resid[at] = first
            total[...] += lax.dot_general(
                stack, stack, (((1,), (1,)), ((), ())), preferred_element_type=F32
            )

    lane1 = lax.broadcasted_iota(jnp.int32, (1, 128), 1)
    local = jnp.zeros((1, 128), F32)
    square = total[0:NZ, 0:NZ] + (total[0:NZ, NZ:] + total[NZ:, 0:NZ]) + total[NZ:, NZ:]
    for k in range(2 * ITERS):
        value = jnp.sum(cheb[k] * square, axis=0, keepdims=True)
        local = jnp.where(lane1 == k, jnp.sum(value, axis=1, keepdims=True), local)
    part[0] = local
    part_z[row] = local
    hops = []
    for dz in range(1, 4):
        copy = pltpu.make_async_remote_copy(
            src_ref=part.at[0],
            dst_ref=part_z.at[row],
            send_sem=z_send.at[dz - 1],
            recv_sem=z_recv.at[dz - 1],
            device_id=(me, lax.rem(row + dz, 4)),
            device_id_type=MESH,
        )
        copy.start()
        hops.append(copy)

    @pl.loop(0, ROWS // 2)
    def _(pair):
        for j in range(ITERS - 1):
            early[j, pair] = times(cheb_ops.at[j], stacks[pair])

    for copy in hops:
        copy.wait()
    along = (part_z[0] + part_z[1]) + (part_z[2] + part_z[3])
    sum_z[0] = along
    part_g[me] = along
    for offset in OFFSETS:
        p = peer(offset)
        pltpu.make_async_remote_copy(
            src_ref=sum_z.at[0],
            dst_ref=part_g.at[me],
            send_sem=g_send.at[0],
            recv_sem=g_recv.at[0],
            device_id=(p, row),
            device_id_type=MESH,
        ).start()
    everyone = pltpu.make_async_remote_copy(
        src_ref=part_g.at[pl.ds(0, FAR)],
        dst_ref=part_g.at[pl.ds(0, FAR)],
        send_sem=g_send.at[0],
        recv_sem=g_recv.at[0],
        device_id=(peer(OFFSETS[0]), row),
        device_id_type=MESH,
    )
    everyone.wait_recv()
    whole = jnp.sum(part_g[...], axis=0)
    moments = [
        jnp.broadcast_to(
            jnp.sum(jnp.where(lane1 == k, whole, 0.0), axis=1, keepdims=True), (1, 128)
        )
        for k in range(2 * ITERS)
    ]
    weights = cg_weights(moments, centre, half)

    def put_back(c, pair, step):
        moved = columns(c, pair) + step
        for r in range(2):
            back[c, pl.ds(pair * 2 + r, NZ, stride=ROWS), :] = moved[:, r * 128 : (r + 1) * 128]

    def send_back(c):
        solved[c, own, :] = back[c, own, :]
        send_chunk(back, solved, c, back_sem, ret_sem)

    wide = [jnp.concatenate([weight, weight], axis=1) for weight in weights]

    @pl.loop(0, ROWS // 2)
    def _(pair):
        step = wide[0] * resid[pair]
        for j in range(1, ITERS):
            step = step + wide[j] * early[j - 1, pair]
        put_back(0, pair, step)

    send_back(0)
    poly = weights[0] * cheb[0]
    for j in range(1, ITERS):
        poly = poly + weights[j] * cheb[j]
    put_ops(step_ops, poly)

    @pl.loop(1, CHUNKS)
    def _(c):
        @pl.loop(0, ROWS // 2)
        def _(pair):
            put_back(c, pair, times(step_ops, stacks[c * (ROWS // 2) + pair]))

        send_back(c)

    @pl.loop(0, CHUNKS)
    def _(c):
        chunk_copy(back, solved, c, back_sem, ret_sem).wait_recv()

        @pl.loop(0, TILES)
        def _(b):
            upper = jnp.full((ROWS, 128), mask_ref[2 * row + 1, b], jnp.int32) != 0
            for d in range(DEPTHS):
                low = pl.ds(pl.multiple_of(b * XT + c * ROWS, ROWS), ROWS)
                high = pl.ds(pl.multiple_of(b * XT + c * ROWS + XT // 2, ROWS), ROWS)
                prior[d, low, :], prior[d, high, :] = mix(
                    solved[c, pl.ds(pl.multiple_of(b * PIECE + d * ROWS, ROWS), ROWS), :],
                    prior[d, low, :], prior[d, high, :], upper, lane8,
                )

    everyone.wait_send()
    for c in range(CHUNKS):
        chunk_copy(sent, field, c, send_sem, recv_sem).wait_send()
        chunk_copy(back, solved, c, back_sem, ret_sem).wait_send()


def place_kernel(solved_ref, out_ref, sem):
    part = TILES * XT // 4
    copies = [
        pltpu.make_async_copy(
            solved_ref.at[d, pl.ds(i * part, part)],
            out_ref.at[d, pl.ds(i * part, part)],
            sem.at[d * 4 + i],
        )
        for d in range(DEPTHS)
        for i in range(4)
    ]
    for copy in copies:
        copy.start()
    for copy in copies:
        copy.wait()


def local(init, measured, mask, kernel_index, kernels):
    nx = TILES * XT
    vmem = pl.BlockSpec(memory_space=pltpu.VMEM)
    hbm = pl.BlockSpec(memory_space=pltpu.HBM)
    dma = pltpu.SemaphoreType.DMA
    solved = pl.pallas_call(
        solve_kernel,
        out_shape=jax.ShapeDtypeStruct((DEPTHS, nx, 128), F32),
        in_specs=[hbm] * 5,
        out_specs=vmem,
        scratch_shapes=[
            pltpu.SMEM((NY_BLOCKS, TILES), jnp.int32),
            pltpu.SMEM((VIEWS * ZBANDS, TILES), jnp.int32),
            pltpu.VMEM((VIEWS * ZBANDS, TILES), jnp.int32),
            pltpu.VMEM((NK, TAPS), F32),
            pltpu.VMEM((2 * CHUNKS, VIEWS * NZ, ROWS, 128), F32),
            pltpu.VMEM((CHUNKS, PART, 128), F32),
            pltpu.VMEM((CHUNKS, PART, 128), F32),
            pltpu.VMEM((CHUNKS, PART, 128), F32),
            pltpu.VMEM((CHUNKS, PART, 128), F32),
            pltpu.VMEM((CHUNKS * ROWS // 2, NZ, 256), F32),
            pltpu.VMEM((CHUNKS * ROWS // 2, 2 * NZ, 256), BF16),
            pltpu.VMEM((VIEWS * NZ, 128), F32),
            pltpu.VMEM((NK, 128), F32),
            pltpu.VMEM((VIEWS * NZ, NZ), F32),
            pltpu.VMEM((2 * NZ, VIEWS * NZ), BF16),
            pltpu.VMEM((2 * NZ, 2 * NZ), BF16),
            pltpu.VMEM((2 * NZ, 2 * NZ), BF16),
            pltpu.VMEM((ITERS - 1, 2 * NZ, 2 * NZ), BF16),
            pltpu.VMEM((ITERS - 1, ROWS // 2, NZ, 256), F32),
            pltpu.VMEM((2 * ITERS, NZ, NZ), F32),
            pltpu.VMEM((2 * NZ, 2 * NZ), F32),
            pltpu.VMEM((1, 1, 128), F32),
            pltpu.VMEM((4, 1, 128), F32),
            pltpu.VMEM((TILES, 1, 128), F32),
            pltpu.VMEM((1, 1, 128), F32),
            dma((4,)),
            dma((DEPTHS,)),
            dma((2 * CHUNKS,)),
            dma((CHUNKS,)),
            dma((CHUNKS,)),
            dma((CHUNKS,)),
            dma((CHUNKS,)),
            dma((3,)),
            dma((3,)),
            dma((1,)),
            dma((1,)),
        ],
        compiler_params=pltpu.CompilerParams(
            collective_id=0, has_side_effects=True, vmem_limit_bytes=48 << 20
        ),
        name="solve",
    )(
        init,
        measured.reshape(VIEWS * NZ, XT, YD),
        pltpu.with_memory_space_constraint(mask.T, pltpu.HBM),
        pltpu.with_memory_space_constraint(
            kernel_index.reshape(VIEWS * ZBANDS, TILES), pltpu.HBM
        ),
        pltpu.with_memory_space_constraint(kernels, pltpu.HBM),
    )
    return pl.pallas_call(
        place_kernel,
        out_shape=jax.ShapeDtypeStruct((DEPTHS, nx, 128), F32),
        in_specs=[vmem],
        out_specs=hbm,
        scratch_shapes=[dma((4 * DEPTHS,))],
        compiler_params=pltpu.CompilerParams(vmem_limit_bytes=8 << 20),
        name="place",
    )(solved)


def solution(mesh):
    return jax.shard_map(
        local,
        mesh=mesh,
        in_specs=(P("gz", None, "gy"), P(None, None, "gz", "gy"), P(), P(), P()),
        out_specs=P("gz", None, "gy"),
        check_vma=False,
    )
```
